32 devices in a mesh: expert: 4 (over z), dp: 8 (over y, x, core).
Axes of the slice: x: 2, y: 2, z: 4, core: 2. Of those that a mesh axis runs over, the one named last changes fastest.
Arguments:
- tokens: bfloat16 [3072, 2304], P(('expert', 'dp')), may hold values from -6 to 6
- expert_ids: int32 [3072, 2], P(('expert', 'dp')), may hold values from 0 to 3, all different within a row; in each aligned block of 96 rows (0 to 95, 96 to 191, ...) at most 64 rows name the same one
- gate_weights: float32 [3072, 2], P(('expert', 'dp')), may hold values from 0.2 to 1
- request_lengths: int32 [32, 4], P(('expert', 'dp')), may hold values from 1 to 48, 96 in all within a row
- request_adapter: int32 [32, 4], P(('expert', 'dp')), may hold values from 0 to 63
- expert_weights: bfloat16 [4, 2, 2304, 5760], P('expert', None, None, 'dp'), may hold values from -0.125 to 0.125
- expert_down: bfloat16 [4, 5760, 2304], P('expert', 'dp'), may hold values from -0.078125 to 0.078125
- low_down: bfloat16 [4, 2304, 2048], P('expert', None, 'dp'), may hold values from -0.125 to 0.125
- low_up: bfloat16 [4, 2, 1024, 5760], P('expert', None, None, 'dp'), may hold values from -1.5 to 1.5
Outputs:
- mixed: bfloat16 [3072, 2304], P(('expert', 'dp'))
The draws below stay inside these ranges and needn't reach their ends.
Inputs may be any that keep to these rules, and one draw needn't show every extreme that they name: `expert_ids`: each row names 2 different experts; within the rows of one device no expert is named by more than 64 rows, a bound that some block reaches. `request_lengths`: each row sums to 96, and its largest entry is exactly 48.
All inputs are finite; a program needn't handle non-finite values.
Results may differ from the reference program's by a relative error of at most 0.017.
Values may be sent and summed in bfloat16 or wider, within the bound.
No kernel may reach another device: no remote copies, remote signals or barrier semaphores. Data moves between devices by JAX's collectives and lax.ppermute only.
A program may use at most 192 MiB of HBM per device.

```python
import math
import jax
import jax.numpy as jnp
import numpy as np
from jax import lax

D = 2304
HIDDEN_UNITS = 5760
TOP = 2
RANK = 16
ADAPTERS = 64
REQ_DEV = 4
TOK_DEV = 96
EXPERTS = 4
EXPERT_CAPACITY = 64
TOKENS = 3072
N_DP = 8
DEVICES = 32


def touch_ends(entries, own_key, least, high):
    longest = entries.shape.index(max(entries.shape))
    spots = []
    for shift in (0, 1):
        where = [jax.random.randint(jax.random.fold_in(own_key, axis), (), 0, length) for axis, length in enumerate(entries.shape)]
        where[longest] = (where[longest] + shift) % entries.shape[longest]
        spots.append(tuple(where))
    return entries.at[spots[0]].set(least).at[spots[1]].set(high)


def steps_of(own_key, shape, cuts, smallest, largest):
    level = 1.0
    for position, parts in cuts:
        steps = jax.random.uniform(jax.random.fold_in(jax.random.fold_in(own_key, 6), position), (parts,), jnp.float32, smallest / len(cuts), largest / len(cuts))
        level = level * jnp.repeat(jnp.exp(steps), shape[position] // parts).reshape((-1,) + (1,) * (len(shape) - 1 - position))
    return level


def rank_bounds(number_of, lean):
    portions = [(1 << 20) // math.isqrt(grade ** lean) + 1 for grade in range(1, number_of + 1)]
    width = 1 + sum(portions) // (1 << 30)
    return np.cumsum(np.array([max(1, weight // width) for weight in portions]))


def skewed_ids(stream_key, shape, count, slope):
    table = rank_bounds(count, slope)
    lot = jax.random.randint(jax.random.fold_in(stream_key, 1), shape, 0, int(table[count - 1]))
    rank = jnp.searchsorted(jnp.asarray(table, jnp.int32), lot, side="right")
    return jax.random.permutation(jax.random.fold_in(stream_key, 2), count)[rank].astype(jnp.int32)


def split_up(number_of, total, most, skew):
    portions = [(1 << 20) // math.isqrt(rank ** skew) + 1 for rank in range(2, number_of + 1)]
    spare, given = total - most - (number_of - 1), [1] * (number_of - 1)
    while spare > 0:
        free = [i for i in range(number_of - 1) if given[i] < most]
        whole, budget = sum([portions[i] for i in free]), spare
        for i in free:
            addition = min(most - given[i], max(1, budget * portions[i] // whole), spare)
            given[i] = given[i] + addition
            spare = spare - addition
    return np.array([most] + given)


def ragged_sizes(key, amount, total, limit, lean):
    if amount == 2:
        one = jax.random.randint(key, (), max(1, total - limit), min(limit, total - 1) + 1)
        return jnp.stack([one, total - one])
    lengths = jnp.asarray(split_up(amount, total, limit, lean), jnp.int32)
    couples = (amount - 1) // 2
    source_of, receiver = lengths[1:1 + 2 * couples:2], lengths[2:2 + 2 * couples:2]
    room = jnp.minimum(source_of - 1, limit - receiver)
    moved = jax.random.randint(jax.random.fold_in(key, 1), (couples,), 0, 1 << 20) % (room + 1)
    lengths = lengths.at[1:1 + 2 * couples:2].set(source_of - moved).at[2:2 + 2 * couples:2].set(receiver + moved)
    return lengths[jax.random.permutation(jax.random.fold_in(key, 2), amount)]


def routed_block(own_key, own, number, rows, number_of, top, bound, lean):
    sequence = jax.random.permutation(own_key, number_of)
    heavy_load, ordinary = shares(number_of, rows * top, bound, lean, True), shares(number_of, rows * top, bound, lean, False)
    places = jnp.arange(number_of)

    def named(sizes, turn):
        used = int((sizes > 0).sum())
        fixed = max(1, used // 4)
        moved = fixed + (places - fixed + turn * (used - fixed)) % max(1, number_of - fixed)
        return jnp.zeros((number_of,), jnp.int32).at[sequence[jnp.where(places < fixed, places, moved)]].set(jnp.asarray(sizes, jnp.int32))

    sizes = jnp.where(number % 4 == 0, named(heavy_load, number // 4), named(ordinary, number - number // 4 - 1))
    mixed = jax.random.permutation(jax.random.fold_in(own, 3), number_of)
    giver, taker = mixed[0:number_of // 2 * 2:2], mixed[1:number_of // 2 * 2:2]
    room = jnp.minimum(sizes[giver] - 1, bound - sizes[taker]) // 2
    room = jnp.where((giver == sequence[0]) | (taker == sequence[0]) | (sizes[taker] == 0), 0, jnp.maximum(room, 0))
    moved = jax.random.randint(jax.random.fold_in(own, 4), (number_of // 2,), 0, 1 << 20) % (room + 1)
    sizes = sizes.at[giver].add(-moved).at[taker].add(moved)
    labels = jnp.searchsorted(jnp.cumsum(sizes), jnp.arange(rows * top), side="right").astype(jnp.int32)
    listing = labels.reshape(top, rows).T
    listing = listing[jax.random.permutation(jax.random.fold_in(own, 1), rows)]
    turn = jax.random.randint(jax.random.fold_in(own, 2), (rows, 1), 0, top)
    return jnp.take_along_axis(listing, (jnp.arange(top)[None, :] + turn) % top, axis=1)


def shares(number_of, total, limit, slope, full):
    portions = [(1 << 20) // math.isqrt(rank ** slope) + 1 for rank in range(1, number_of + 1)]
    largest = limit if full else min(limit, max(-(-total // number_of), total * portions[0] // sum(portions)))
    least = 1 if total - largest >= number_of - 1 else 0
    counts, spare = [largest] + [least] * (number_of - 1), total - largest - least * (number_of - 1)
    while spare > 0:
        movable = [i for i in range(1, number_of) if counts[i] < largest] or [i for i in range(1, number_of) if counts[i] < limit]
        pool, budget = sum([portions[i] for i in movable]), spare
        for i in movable:
            more = min(limit - counts[i], max(1, budget * portions[i] // pool), spare)
            counts[i] = counts[i] + more
            spare = spare - more
    return np.array(counts)


def bell_draw(rng, dims, scale, limit, cuts=(), kind=jnp.bfloat16):
    loudness = steps_of(rng, dims, cuts, -0.22, 0.18) if cuts else 1.0
    entries = jax.random.normal(rng, dims, jnp.float32) * scale * loudness
    return jnp.minimum(jnp.maximum(entries, -limit), limit).astype(kind)


def setup_inputs(seed: int = 0) -> dict:
    keys = jax.random.split(jax.random.key(seed), 10)
    tokens = bell_draw(keys[0], (TOKENS, D), 1.0, 6.0, ((0, 32),))
    expert_ids_keys = jax.random.split(jax.random.fold_in(keys[1], 1), TOKENS // TOK_DEV)
    expert_ids_turns = jax.random.permutation(jax.random.fold_in(keys[1], 3), TOKENS // TOK_DEV)
    expert_ids = jax.vmap(lambda own, number: routed_block(jax.random.fold_in(keys[1], 2), own, number, TOK_DEV, EXPERTS, TOP, EXPERT_CAPACITY, 1))(expert_ids_keys, expert_ids_turns).reshape((TOKENS, TOP))
    gate_weights = jnp.clip(0.2 + 0.8 * jax.random.uniform(keys[2], (TOKENS, TOP), jnp.float32) ** steps_of(keys[2], (TOKENS, TOP), ((0, 32),), -0.2, 0.2), 0.2, 1.0)
    request_lengths = jax.vmap(lambda own: ragged_sizes(own, REQ_DEV, TOK_DEV, TOK_DEV // 2, 2))(jax.random.split(keys[3], DEVICES)).reshape((DEVICES, REQ_DEV)).astype(jnp.int32)
    request_adapter = touch_ends(skewed_ids(keys[4], (DEVICES, REQ_DEV), ADAPTERS, 2), jax.random.fold_in(keys[4], 3), 0, ADAPTERS - 1).astype(jnp.int32)
    expert_weights = bell_draw(keys[5], (EXPERTS, 2, D, HIDDEN_UNITS), D ** -0.5, 0.125, ((0, 4), (3, 8)))
    expert_down = bell_draw(keys[6], (EXPERTS, HIDDEN_UNITS, D), HIDDEN_UNITS ** -0.5, 0.078125, ((0, 4), (1, 8)))
    low_down = bell_draw(keys[7], (EXPERTS, D, ADAPTERS * 2 * RANK), D ** -0.5, 0.125, ((0, 4), (2, 8)))
    low_up = bell_draw(keys[8], (EXPERTS, 2, ADAPTERS * RANK, HIDDEN_UNITS), RANK ** -0.5, 1.5, ((0, 4), (3, 8)))
    return dict(tokens=tokens, expert_ids=expert_ids, gate_weights=gate_weights, request_lengths=request_lengths, request_adapter=request_adapter, expert_weights=expert_weights, expert_down=expert_down, low_down=low_down, low_up=low_up)


def token_adapters(request_lengths, request_adapter):
    ends = jnp.cumsum(request_lengths, axis=1)
    place = jnp.arange(TOK_DEV, dtype=jnp.int32)
    which = lax.optimization_barrier(jnp.sum((place[None, :, None] >= ends[:, None, :]).astype(jnp.int32), axis=2))
    return jnp.take_along_axis(request_adapter, which, axis=1).reshape(-1)

def slots_of(flat):
    onehot = (flat[:, :, None] == jnp.arange(EXPERTS, dtype=jnp.int32)[None, None, :]).astype(jnp.int32)
    before = jnp.cumsum(onehot, axis=1) - onehot
    return lax.optimization_barrier(jnp.sum(before * onehot, axis=2))

def expert_block(rows, tags, weights, down_weight_blocks, down_low, up_low):
    chosen = down_low[:, tags, :]
    lowrank = jnp.einsum('cd,dck->ck', rows.astype(jnp.float32), chosen).astype(jnp.bfloat16)
    lifted = up_low[:, tags]
    lowf = lowrank.astype(jnp.float32)
    gate = jnp.dot(rows, weights[0], preferred_element_type=jnp.float32) + jnp.einsum('cr,crf->cf', lowf[:, :RANK], lifted[0])
    up = jnp.dot(rows, weights[1], preferred_element_type=jnp.float32) + jnp.einsum('cr,crf->cf', lowf[:, RANK:], lifted[1])
    hidden_activations = (jax.nn.silu(gate) * up).astype(jnp.bfloat16)
    partial_pieces = jnp.einsum('ert,rtj->erj', hidden_activations.astype(jnp.float32).reshape(EXPERT_CAPACITY, N_DP, HIDDEN_UNITS // N_DP), down_weight_blocks)
    partial_pieces = lax.optimization_barrier(partial_pieces.astype(jnp.bfloat16))
    return lax.optimization_barrier(jnp.sum(partial_pieces.astype(jnp.float32), axis=1)).astype(jnp.bfloat16)

def reference(tokens, expert_ids, gate_weights, request_lengths, request_adapter, expert_weights, expert_down, low_down, low_up):
    values = tokens.astype(jnp.float32)
    normed = (values * lax.rsqrt(lax.optimization_barrier(jnp.mean(values * values, axis=1, keepdims=True)) + 1e-05)).astype(jnp.bfloat16)
    adapter = token_adapters(request_lengths, request_adapter)
    flat = expert_ids.reshape(DEVICES, TOK_DEV * TOP)
    slot = slots_of(flat)
    where_dev = jnp.arange(DEVICES, dtype=jnp.int32)[:, None] * EXPERT_CAPACITY + slot
    pairs = jnp.repeat(normed, TOP, axis=0)
    pair_adapter = jnp.repeat(adapter, TOP).astype(jnp.int32)
    dump = DEVICES * EXPERT_CAPACITY

    def one_expert(inputs):
        index, weights, down, ldown, lup = inputs
        target = jnp.where(flat == index, where_dev, dump).reshape(-1).astype(jnp.int32)
        rows = jnp.zeros((dump + 1, D), jnp.bfloat16).at[target].set(pairs)[:dump]
        tags = jnp.zeros((dump + 1,), jnp.int32).at[target].set(pair_adapter)[:dump]
        down_weight_blocks = down.astype(jnp.float32).reshape(N_DP, HIDDEN_UNITS // N_DP, D)
        down_low = ldown.astype(jnp.float32).reshape(D, ADAPTERS, 2 * RANK)
        up_low = lup.astype(jnp.float32).reshape(2, ADAPTERS, RANK, HIDDEN_UNITS)

        def per_device(item):
            return expert_block(item[0], item[1], weights, down_weight_blocks, down_low, up_low)
        done = lax.map(per_device, (rows.reshape(DEVICES, EXPERT_CAPACITY, D), tags.reshape(DEVICES, EXPERT_CAPACITY)))
        return done.reshape(dump, D)
    outs = lax.map(one_expert, (jnp.arange(EXPERTS, dtype=jnp.int32), expert_weights, expert_down, low_down, low_up))
    index = (flat * dump + where_dev).reshape(-1).astype(jnp.int32)
    got = outs.reshape(EXPERTS * dump, D)[index].reshape(TOKENS, TOP, D)
    mixed = values + lax.optimization_barrier(jnp.sum(gate_weights[:, :, None] * got.astype(jnp.float32), axis=1))
    return mixed.astype(jnp.bfloat16)
```

```python
import jax
import jax.numpy as jnp
from jax import lax
from jax.sharding import PartitionSpec as P

TOP = 2
RANK = 16
LANES = 128
BF = jnp.bfloat16
F32 = jnp.float32


def swap(x, axis, bit):
    n = lax.axis_size(axis)
    return lax.ppermute(x, axis, [(i, i ^ bit) for i in range(n)])


def gather_rows(own, bits):
    pieces = {0: own}
    if len(bits) == 2:
        bx, by = bits
        half = own.shape[0] // 2
        px = swap(own, "dp", bx)
        py = swap(own, "dp", by)
        low = swap(px[:half], "dp", by)
        high = swap(py[half:], "dp", bx)
        return [own, px, py, jnp.concatenate([low, high], axis=0)]
    for b in bits:
        for p in list(pieces):
            pieces[p ^ b] = swap(pieces[p], "dp", b)
    return [pieces[p] for p in positions(bits)]


def positions(bits):
    out = [0]
    for b in bits:
        out = out + [p ^ b for p in out]
    return out


def reduce_rows(parts, bits):
    if len(bits) == 2:
        bx, by = bits
        s0, sx, sy, sd = parts
        half = s0.shape[0] // 2
        low = swap(sd[:half], "dp", bx)
        high = swap(sd[half:], "dp", by)
        sy = jnp.concatenate(
            [(sy[:half].astype(F32) + low.astype(F32)).astype(BF), sy[half:]], axis=0
        )
        sx = jnp.concatenate(
            [sx[:half], (sx[half:].astype(F32) + high.astype(F32)).astype(BF)], axis=0
        )
        rx = swap(sx, "dp", bx)
        ry = swap(sy, "dp", by)
        return (s0.astype(F32) + rx.astype(F32) + ry.astype(F32)).astype(BF)
    pos = positions(bits)
    table = dict(zip(pos, parts))
    for b in reversed(bits):
        keep = [p for p in table if not p & b]
        table = {
            p: (table[p].astype(F32) + swap(table[p ^ b], "dp", b).astype(F32)).astype(BF)
            for p in keep
        }
    return table[0]


def body(
    tokens,
    expert_ids,
    gate_weights,
    request_lengths,
    request_adapter,
    expert_weights,
    expert_down,
    low_down,
    low_up,
):
    experts = lax.axis_size("expert")
    n_dp = lax.axis_size("dp")
    local_tokens, width = tokens.shape
    capacity = local_tokens * TOP * 4 // (3 * experts)
    held = low_down.shape[2] // (2 * RANK)
    adapters_all = low_up.shape[2] // RANK
    bits = []
    b = 2
    while b < n_dp:
        bits.append(b)
        b *= 2
    z = lax.axis_index("expert")
    me = lax.axis_index("dp")

    ld = (low_down[0], swap(low_down[0], "dp", 1))
    wt = (expert_weights[0], swap(expert_weights[0], "dp", 1))
    lu = (low_up[0], swap(low_up[0], "dp", 1))
    dn = (expert_down[0], swap(expert_down[0], "dp", 1))

    values = tokens.astype(F32)
    normed = (
        values * lax.rsqrt(jnp.mean(values * values, axis=1, keepdims=True) + 1e-05)
    ).astype(BF)
    place = jnp.arange(local_tokens, dtype=jnp.int32)
    ends = jnp.sum(
        jnp.where(
            jnp.arange(4)[:, None] <= jnp.arange(4)[None, :], request_lengths[0][:, None], 0
        ),
        axis=0,
    )
    which = jnp.sum((place[:, None] >= ends[None, :]).astype(jnp.int32), axis=1)
    lookup = which[:, None] == jnp.arange(request_lengths.shape[1], dtype=jnp.int32)[None, :]
    adapter = jnp.sum(jnp.where(lookup, request_adapter, 0), axis=1)
    tag = jnp.where(
        jnp.arange(LANES)[None, :] == 0, adapter[:, None].astype(BF), jnp.zeros((), BF)
    )
    ext = jnp.concatenate([normed, tag], axis=1)

    want = jnp.arange(experts, dtype=jnp.int32) ^ z
    ids_t = expert_ids.T
    member = (ids_t[0][None, :] == want[:, None]) | (ids_t[1][None, :] == want[:, None])
    before = (place[:, None] < place[None, :]).astype(BF)
    slot = jnp.dot(member.astype(BF), before, preferred_element_type=F32).astype(jnp.int32)
    put = (
        (jnp.arange(capacity, dtype=jnp.int32)[None, :, None] == slot[:, None, :])
        & member[:, None, :]
    ).astype(BF)
    outgoing = jnp.dot(
        put.reshape(experts * capacity, local_tokens), ext, preferred_element_type=F32
    ).astype(BF)
    outgoing = outgoing.reshape(experts, capacity, width + LANES)

    chunks = [[d] for d in range(experts)]
    arrived = [outgoing[0]] + [swap(outgoing[d], "expert", d) for d in range(1, experts)]
    total = jnp.zeros((local_tokens, width), F32)
    for chunk in chunks:
        own = jnp.concatenate([arrived[d] for d in chunk], axis=0)
        ext_rows = jnp.concatenate(gather_rows(own, bits), axis=0)
        rows = ext_rows[:, :width]
        labels = ext_rows[:, width].astype(jnp.int32)
        count = rows.shape[0]
        part = jnp.zeros((count, 2 * RANK), F32)
        for side in range(2):
            projected = jnp.dot(rows, ld[side], preferred_element_type=F32).reshape(
                count, held, 2 * RANK
            )
            owned = labels[:, None] == (me ^ side) * held + jnp.arange(held, dtype=jnp.int32)[None, :]
            part = part + jnp.sum(jnp.where(owned[:, :, None], projected, 0.0), axis=1)
        lowrank = part.astype(BF)
        group = count // (2 ** len(bits))
        pos = positions(bits)
        for b in bits:
            other = swap(lowrank, "dp", b).reshape(len(pos), group, 2 * RANK)
            other = jnp.stack([other[pos.index(p ^ b)] for p in pos])
            lowrank = lowrank + other.reshape(count, 2 * RANK)
        marks = (
            labels[:, None] == jnp.arange(adapters_all, dtype=jnp.int32)[None, :]
        ).astype(BF)
        spread = [
            (marks[:, :, None] * lowrank[:, None, g * RANK : (g + 1) * RANK]).reshape(
                count, adapters_all * RANK
            )
            for g in range(2)
        ]
        out = jnp.zeros((count, width), F32)
        for side in range(2):
            act = [
                jnp.dot(rows, wt[side][g], preferred_element_type=F32)
                + jnp.dot(spread[g], lu[side][g], preferred_element_type=F32)
                for g in range(2)
            ]
            hidden = (jax.nn.silu(act[0]) * act[1]).astype(BF)
            out = out + jnp.dot(hidden, dn[side], preferred_element_type=F32)
        out = out.astype(BF).reshape(len(pos), group, width)
        done = reduce_rows([out[i] for i in range(len(pos))], bits)
        for i, d in enumerate(chunk):
            piece = done[i * capacity : (i + 1) * capacity]
            back = piece if d == 0 else swap(piece, "expert", d)
            scale = jnp.sum(jnp.where(expert_ids == (z ^ d), gate_weights, 0.0), axis=1)
            total = total + scale[:, None] * jnp.dot(
                put[d].T, back, preferred_element_type=F32
            )
    return (values + total).astype(BF)


def solution(mesh):
    return jax.shard_map(
        body,
        mesh=mesh,
        in_specs=(
            P(("expert", "dp"), None),
            P(("expert", "dp"), None),
            P(("expert", "dp"), None),
            P(("expert", "dp"), None),
            P(("expert", "dp"), None),
            P("expert", None, None, "dp"),
            P("expert", "dp", None),
            P("expert", None, "dp"),
            P("expert", None, None, "dp"),
        ),
        out_specs=P(("expert", "dp"), None),
        check_vma=False,
    )
```

```python
import functools

import jax
import jax.numpy as jnp
from jax import lax
from jax.experimental import pallas as pl
from jax.experimental.pallas import tpu as pltpu
from jax.sharding import PartitionSpec as P

TOP = 2
RANK = 16
LANES = 128
BF = jnp.bfloat16
F32 = jnp.float32
I32 = jnp.int32
VM = pl.BlockSpec(memory_space=pltpu.VMEM)
SM = pl.BlockSpec(memory_space=pltpu.SMEM)


def swap(x, axis, bit):
    n = lax.axis_size(axis)
    return lax.ppermute(x, axis, [(i, i ^ bit) for i in range(n)])


def call(fn, outs, args, specs, flops, name):
    size = sum(a.size * a.dtype.itemsize for a in args) + sum(
        o.size * o.dtype.itemsize for o in outs
    )
    return pl.pallas_call(
        fn,
        out_shape=tuple(outs),
        in_specs=specs,
        out_specs=tuple(VM for _ in outs),
        compiler_params=pltpu.CompilerParams(vmem_limit_bytes=16 << 20),
        cost_estimate=pl.CostEstimate(flops=flops, bytes_accessed=size, transcendentals=0),
        name=name,
    )(*args)


def shape(rows, cols, dtype=BF):
    return jax.ShapeDtypeStruct((rows, cols), dtype)


def one_hots(ids_ref, z, experts, capacity, local_tokens):
    first = ids_ref[0:1, :]
    second = ids_ref[1:2, :]
    member = jnp.concatenate(
        [((first == (z ^ d)) | (second == (z ^ d))).astype(F32) for d in range(experts)], axis=0
    )
    before = (
        lax.broadcasted_iota(I32, (local_tokens, local_tokens), 0)
        < lax.broadcasted_iota(I32, (local_tokens, local_tokens), 1)
    ).astype(F32)
    slot = jnp.dot(member.astype(BF), before.astype(BF), preferred_element_type=F32)
    rank = lax.broadcasted_iota(I32, (capacity, local_tokens), 0).astype(F32)
    return [
        jnp.where((rank == slot[d : d + 1, :]) & (member[d : d + 1, :] > 0.0), 1.0, 0.0)
        for d in range(experts)
    ]


def front_kernel(experts, capacity, z_ref, len_ref, ada_ref, ids_ref, tok_ref, *outs):
    local_tokens, width = tok_ref.shape
    values = tok_ref[...].astype(F32)
    normed = (
        values * lax.rsqrt(jnp.mean(values * values, axis=1, keepdims=True) + 1e-05)
    ).astype(BF)
    place = lax.broadcasted_iota(I32, (local_tokens, LANES), 0)
    lane = lax.broadcasted_iota(I32, (local_tokens, LANES), 1)
    tag = jnp.zeros((local_tokens, LANES), F32) + ada_ref[0, 0].astype(F32)
    end = len_ref[0, 0]
    for r in range(1, len_ref.shape[1]):
        tag = jnp.where(place >= end, ada_ref[0, r].astype(F32), tag)
        end = end + len_ref[0, r]
    tag = jnp.where(lane == 0, tag, 0.0).astype(BF)
    puts = one_hots(ids_ref, z_ref[0], experts, capacity, local_tokens)
    for d in range(experts):
        put = puts[d].astype(BF)
        outs[d][:, :width] = jnp.dot(put, normed, preferred_element_type=F32).astype(BF)
        outs[d][:, width:] = jnp.dot(put, tag, preferred_element_type=F32).astype(BF)


def proj_kernel(counts, held, me_ref, fold_ref, *refs):
    n = sum(counts)
    piece_refs = refs[:n]
    ld_refs = refs[n : n + 2]
    rows_ref, tag_ref = refs[n + 2], refs[n + 3]
    packs = refs[n + 4 :]
    width = rows_ref.shape[1]
    start = 0
    for ref in piece_refs:
        size = ref.shape[0]
        rows_ref[start : start + size, :] = ref[:, :width]
        tag_ref[start : start + size, :] = ref[:, width:]
        start += size
    spots = len(counts)
    group = start // spots
    labels = tag_ref[:, 0:1].astype(F32)
    cols = held * 2 * RANK
    column = lax.broadcasted_iota(I32, (1, cols), 1) // (2 * RANK)
    kept = []
    for side in range(2):
        base = (me_ref[0] ^ side) * held
        prod = jnp.dot(rows_ref[...], ld_refs[side][...], preferred_element_type=F32)
        kept.append(jnp.where(labels == (column + base).astype(F32), prod, 0.0).astype(BF))
    folded = jnp.dot(kept[0] + kept[1], fold_ref[...], preferred_element_type=F32)
    lanes = packs[0].shape[1]
    spot = lax.broadcasted_iota(I32, (1, lanes), 1) // (2 * RANK)
    for s in range(spots):
        total = jnp.zeros((group, lanes), F32)
        for p in range(spots):
            total = total + jnp.where(
                spot == (p ^ s), folded[p * group : (p + 1) * group, :], 0.0
            )
        packs[s][...] = total.astype(BF)


def nt(a, b):
    return lax.dot_general(a, b, (((1,), (1,)), ((), ())), preferred_element_type=F32)


def main_kernel(rows_ref, own_ref, par_ref, raw_ref):
    for side, ref in enumerate((own_ref, par_ref)):
        for g in range(2):
            raw_ref[2 * side + g, :, :] = nt(rows_ref[...], ref[g, :, :])


def down_kernel(spots, adapters, tile_ref, *refs):
    packs = refs[:spots]
    tag_ref, raw_ref = refs[spots], refs[spots + 1]
    lu_refs = refs[spots + 2 : spots + 4]
    dn_refs = refs[spots + 4 : spots + 6]
    outs = refs[spots + 6 :]
    lanes = packs[0].shape[1]
    low = packs[0][...].astype(F32)
    for s in range(1, spots):
        low = low + packs[s][...].astype(F32)
    spot = lax.broadcasted_iota(I32, (1, lanes), 1) // (2 * RANK)
    low = jnp.concatenate(
        [jnp.where(spot == p, low, 0.0).astype(BF) for p in range(spots)], axis=0
    )
    labels = tag_ref[:, 0:1].astype(F32)
    wide = adapters * RANK
    owner = (lax.broadcasted_iota(I32, (1, wide), 1) // RANK).astype(F32)
    mark = labels == owner
    spread = [
        jnp.where(
            mark, jnp.dot(low, tile_ref[g, :, :], preferred_element_type=F32), 0.0
        ).astype(BF)
        for g in range(2)
    ]
    total = None
    for side in range(2):
        act = [
            raw_ref[2 * side + g, :, :] + nt(spread[g], lu_refs[side][g, :, :])
            for g in range(2)
        ]
        hidden = (act[0] / (1.0 + jnp.exp(-act[0])) * act[1]).astype(BF)
        term = jnp.dot(hidden, dn_refs[side][...], preferred_element_type=F32)
        total = term if total is None else total + term
    start = 0
    for ref in outs:
        ref[...] = total[start : start + ref.shape[0], :].astype(BF)
        start += ref.shape[0]


def add_kernel(a_ref, b_ref, o_ref):
    o_ref[...] = (a_ref[...].astype(F32) + b_ref[...].astype(F32)).astype(BF)


def add_rows(a, b):
    return call(add_kernel, [shape(*a.shape)], (a, b), [VM, VM], a.size, "add_rows")[0]


def sum_kernel(s_ref, xl_ref, xh_ref, yl_ref, yh_ref, o_ref):
    half = xl_ref.shape[0]
    o_ref[:half, :] = (
        s_ref[:half, :].astype(F32) + xl_ref[...].astype(F32) + yl_ref[...].astype(F32)
    ).astype(BF)
    o_ref[half:, :] = (
        s_ref[half:, :].astype(F32) + xh_ref[...].astype(F32) + yh_ref[...].astype(F32)
    ).astype(BF)


def back_kernel(experts, capacity, z_ref, ids_ref, idc_ref, gw_ref, tok_ref, *refs):
    backs = refs[:-1]
    out_ref = refs[-1]
    local_tokens = tok_ref.shape[0]
    puts = one_hots(ids_ref, z_ref[0], experts, capacity, local_tokens)
    total = None
    for d in range(experts):
        scale = jnp.sum(
            jnp.where(idc_ref[...] == (z_ref[0] ^ d), gw_ref[...], 0.0), axis=1, keepdims=True
        )
        got = lax.dot_general(
            puts[d].astype(BF),
            backs[d][...],
            (((0,), (0,)), ((), ())),
            preferred_element_type=F32,
        )
        total = scale * got if total is None else total + scale * got
    out_ref[...] = (tok_ref[...].astype(F32) + total).astype(BF)


def positions(bits):
    out = [0]
    for b in bits:
        out = out + [p ^ b for p in out]
    return out


def after(values, deps):
    return lax.optimization_barrier((values, deps))[0]


def gather_first(own, bits):
    if len(bits) == 2:
        return own, swap(own, "dp", bits[0]), swap(own, "dp", bits[1])
    return (own,)


def gather_second(have, bits):
    if len(bits) == 2:
        own, px, py = have
        half = own.shape[0] // 2
        low = swap(px[:half], "dp", bits[1])
        high = swap(py[half:], "dp", bits[0])
        return (own, px, py, low, high), [1, 1, 1, 2]
    pieces = {0: have[0]}
    for b in bits:
        for p in list(pieces):
            pieces[p ^ b] = swap(pieces[p], "dp", b)
    return tuple(pieces[p] for p in positions(bits)), [1] * (2 ** len(bits))


def split_sizes(group, bits):
    if len(bits) == 2:
        half = group // 2
        return [group] + [half] * 6
    return [group] * (2 ** len(bits))


def reduce_first(parts, bits):
    if len(bits) == 2:
        bx, by = bits
        s0, xl, xh, yl, yh, dl, dh = parts
        gl = swap(dl, "dp", bx)
        gh = swap(dh, "dp", by)
        rxl = swap(xl, "dp", bx)
        ryh = swap(yh, "dp", by)
        return s0, rxl, add_rows(xh, gh), add_rows(yl, gl), ryh
    return tuple(parts)


def reduce_second(parts, bits):
    if len(bits) == 2:
        bx, by = bits
        s0, rxl, xh, yl, ryh = parts
        rxh = swap(xh, "dp", bx)
        ryl = swap(yl, "dp", by)
        return call(
            sum_kernel, [shape(*s0.shape)], (s0, rxl, rxh, ryl, ryh), [VM] * 5, s0.size, "sum_rows"
        )[0]
    table = dict(zip(positions(bits), parts))
    for b in reversed(bits):
        keep = [p for p in table if not p & b]
        table = {p: add_rows(table[p], swap(table[p ^ b], "dp", b)) for p in keep}
    return table[0]


def body(
    tokens,
    expert_ids,
    gate_weights,
    request_lengths,
    request_adapter,
    expert_weights,
    expert_down,
    low_down,
    low_up,
):
    experts = lax.axis_size("expert")
    n_dp = lax.axis_size("dp")
    local_tokens, width = tokens.shape
    capacity = local_tokens * TOP * 4 // (3 * experts)
    held = low_down.shape[2] // (2 * RANK)
    adapters = low_up.shape[2] // RANK
    units = expert_down.shape[1]
    bits = []
    b = 2
    while b < n_dp:
        bits.append(b)
        b *= 2
    pos = positions(bits)
    spots = len(pos)
    z = lax.axis_index("expert").astype(I32).reshape(1)
    me = lax.axis_index("dp").astype(I32).reshape(1)
    ids_t = expert_ids.T

    outgoing = call(
        functools.partial(front_kernel, experts, capacity),
        [shape(capacity, width + LANES)] * experts,
        (z, request_lengths, request_adapter, ids_t, tokens),
        [SM, SM, SM, VM, VM],
        2 * experts * capacity * local_tokens * width,
        "front",
    )
    arrived = [outgoing[0]] + [swap(outgoing[d], "expert", d) for d in range(1, experts)]

    wt_t = jnp.swapaxes(expert_weights[0], 1, 2)
    lu_t = jnp.swapaxes(low_up[0], 1, 2)
    ld = (low_down[0], swap(low_down[0], "dp", 1))
    wt = (wt_t, swap(wt_t, "dp", 1))
    lu = (lu_t, swap(lu_t, "dp", 1))
    dn = (expert_down[0], swap(expert_down[0], "dp", 1))
    lanes = 2 * RANK * spots
    fold = (
        jnp.arange(held * 2 * RANK)[:, None] % (2 * RANK) == jnp.arange(lanes)[None, :] % (2 * RANK)
    ).astype(BF)
    tile = jnp.stack(
        [
            (
                jnp.arange(lanes)[:, None] % (2 * RANK)
                == jnp.arange(adapters * RANK)[None, :] % RANK + g * RANK
            ).astype(BF)
            for g in range(2)
        ]
    )

    order = list(range(experts))
    first, second = {}, {}
    parts, done, adds = {}, {}, {}
    first[0] = gather_first(arrived[order[0]], bits)
    second[0] = gather_second(first[0], bits)
    first[1] = gather_first(arrived[order[1]], bits)
    raw = None
    for i, d in enumerate(order):
        pieces, counts = second[i]
        group = capacity
        count = group * spots
        if i == 0:
            pieces, ld, wt = after((pieces, ld, wt), ())
        else:
            pieces = after(pieces, parts[i - 1][0])
        got = call(
            functools.partial(proj_kernel, counts, held),
            [shape(count, width), shape(count, LANES)] + [shape(group, lanes)] * spots,
            (me, fold, *pieces, *ld),
            [SM] + [VM] * (len(pieces) + 3),
            4 * count * width * held * 2 * RANK,
            "project",
        )
        rows, tags, packs = got[0], got[1], got[2:]
        packs = [packs[0]] + [swap(packs[s], "dp", pos[s]) for s in range(1, spots)]
        if i == 0:
            rows, lu, dn = after((rows, lu, dn), ())
        raw = call(
            main_kernel,
            [jax.ShapeDtypeStruct((4, count, units), F32)],
            (rows, *wt),
            [VM] * 3,
            8 * count * width * units,
            "gate_up",
        )[0]
        deps = []
        if i + 1 < experts:
            second[i + 1] = gather_second(first[i + 1], bits)
            deps.append(first[i + 1])
        if i + 2 < experts:
            first[i + 2] = gather_first(arrived[order[i + 2]], bits)
        if i >= 1:
            adds[i - 1] = reduce_first(parts[i - 1], bits)
            deps.append(adds[i - 1])
        if i >= 2:
            done[i - 2] = reduce_second(adds[i - 2], bits)
            deps.append(done[i - 2])
        raw = after(raw, deps)
        parts[i] = call(
            functools.partial(down_kernel, spots, adapters),
            [shape(size, width) for size in split_sizes(group, bits)],
            (tile, *packs, tags, raw, *lu, *dn),
            [VM] * (spots + 7),
            8 * count * adapters * RANK * units + 4 * count * units * width,
            "down",
        )
    for i in range(experts):
        if i not in adds:
            adds[i] = reduce_first(parts[i], bits)
        if i not in done:
            done[i] = reduce_second(adds[i], bits)
    backs = [None] * experts
    for i, d in enumerate(order):
        backs[d] = done[i] if d == 0 else swap(done[i], "expert", d)

    return call(
        functools.partial(back_kernel, experts, capacity),
        [shape(local_tokens, width)],
        (z, ids_t, expert_ids, gate_weights, tokens, *backs),
        [SM] + [VM] * (4 + experts),
        2 * experts * capacity * local_tokens * width,
        "combine",
    )[0]


def solution(mesh):
    return jax.shard_map(
        body,
        mesh=mesh,
        in_specs=(
            P(("expert", "dp"), None),
            P(("expert", "dp"), None),
            P(("expert", "dp"), None),
            P(("expert", "dp"), None),
            P(("expert", "dp"), None),
            P("expert", None, None, "dp"),
            P("expert", "dp", None),
            P("expert", None, "dp"),
            P("expert", None, None, "dp"),
        ),
        out_specs=P(("expert", "dp"), None),
        check_vma=False,
    )
```

```python
import functools

import jax
import jax.numpy as jnp
from jax import lax
from jax.experimental import pallas as pl
from jax.experimental.pallas import tpu as pltpu
from jax.sharding import PartitionSpec as P

TOP = 2
RANK = 16
LANES = 128
COST = 16
BF = jnp.bfloat16
F32 = jnp.float32
I32 = jnp.int32
VM = pl.BlockSpec(memory_space=pltpu.VMEM)
SM = pl.BlockSpec(memory_space=pltpu.SMEM)
ANY = pl.BlockSpec(memory_space=pltpu.HBM)


def swap(x, axis, bit):
    n = lax.axis_size(axis)
    return lax.ppermute(x, axis, [(i, i ^ bit) for i in range(n)])


def spot_mask(index, spot, bits):
    turn = index & 1 if len(bits) == 2 else 0
    mask = 0
    for j in range(len(bits)):
        if spot >> j & 1:
            mask ^= bits[j ^ turn]
    return mask


def hop(x, spot, bits):
    n = lax.axis_size("dp")
    return lax.ppermute(x, "dp", [(i, i ^ spot_mask(i, spot, bits)) for i in range(n)])


def call(fn, outs, args, specs, flops, name, scratch=(), out_spec=VM):
    size = sum(a.size * a.dtype.itemsize for a in args)
    return pl.pallas_call(
        fn,
        out_shape=tuple(outs),
        in_specs=specs,
        out_specs=tuple(out_spec for _ in outs),
        scratch_shapes=scratch,
        compiler_params=pltpu.CompilerParams(vmem_limit_bytes=16 << 20),
        cost_estimate=pl.CostEstimate(
            flops=flops // COST, bytes_accessed=size // COST, transcendentals=0
        ),
        name=name,
    )(*args)


def pin(arrays):
    return [pltpu.with_memory_space_constraint(a, pltpu.HBM) for a in arrays]


def shape(rows, cols, dtype=BF):
    return jax.ShapeDtypeStruct((rows, cols), dtype)


def one_hots(ids_ref, z, experts, capacity, local_tokens):
    first = ids_ref[0:1, :]
    second = ids_ref[1:2, :]
    member = jnp.concatenate(
        [((first == (z ^ d)) | (second == (z ^ d))).astype(F32) for d in range(experts)], axis=0
    )
    before = (
        lax.broadcasted_iota(I32, (local_tokens, local_tokens), 0)
        < lax.broadcasted_iota(I32, (local_tokens, local_tokens), 1)
    ).astype(F32)
    slot = jnp.dot(member.astype(BF), before.astype(BF), preferred_element_type=F32)
    rank = lax.broadcasted_iota(I32, (capacity, local_tokens), 0).astype(F32)
    return [
        jnp.where((rank == slot[d : d + 1, :]) & (member[d : d + 1, :] > 0.0), 1.0, 0.0)
        for d in range(experts)
    ]


def front_kernel(experts, capacity, z_ref, len_hbm, ada_hbm, ids_hbm, tok_hbm, *refs):
    outs = refs[:experts]
    len_ref, ada_ref, ids_ref, tok_ref, put_ref, sems, out_sems = refs[experts:]
    copies = [
        pltpu.make_async_copy(src, dst, sems.at[i])
        for i, (src, dst) in enumerate(
            [(tok_hbm, tok_ref), (ids_hbm, ids_ref), (len_hbm, len_ref), (ada_hbm, ada_ref)]
        )
    ]
    for copy in copies:
        copy.start()
    for copy in copies:
        copy.wait()
    local_tokens, width = tok_ref.shape
    values = tok_ref[...].astype(F32)
    normed = (
        values * lax.rsqrt(jnp.mean(values * values, axis=1, keepdims=True) + 1e-05)
    ).astype(BF)
    place = lax.broadcasted_iota(I32, (local_tokens, LANES), 0)
    lane = lax.broadcasted_iota(I32, (local_tokens, LANES), 1)
    tag = jnp.zeros((local_tokens, LANES), F32) + ada_ref[0, 0].astype(F32)
    end = len_ref[0, 0]
    for r in range(1, len_ref.shape[1]):
        tag = jnp.where(place >= end, ada_ref[0, r].astype(F32), tag)
        end = end + len_ref[0, r]
    tag = jnp.where(lane == 0, tag, 0.0).astype(BF)
    puts = one_hots(ids_ref, z_ref[0], experts, capacity, local_tokens)
    sends = []
    for d in range(experts):
        put = puts[d].astype(BF)
        put_ref[d, :, :width] = jnp.dot(put, normed, preferred_element_type=F32).astype(BF)
        put_ref[d, :, width:] = jnp.dot(put, tag, preferred_element_type=F32).astype(BF)
        sends.append(pltpu.make_async_copy(put_ref.at[d], outs[d], out_sems.at[d]))
        sends[d].start()
    for send in sends:
        send.wait()


def stage_kernel(axis, *refs):
    out_ref, sems = refs[-2:]
    copies = []
    start = 0
    for i, ref in enumerate(refs[:-2]):
        size = ref.shape[axis]
        where = tuple([slice(None)] * axis + [pl.ds(start, size)])
        copies.append(pltpu.make_async_copy(ref, out_ref.at[where], sems.at[i]))
        start += size
    for copy in copies:
        copy.start()
    for copy in copies:
        copy.wait()


def stage(arrays, axis, name):
    dims = list(arrays[0].shape)
    dims[axis] = sum(a.shape[axis] for a in arrays)
    return pl.pallas_call(
        functools.partial(stage_kernel, axis),
        out_shape=pltpu.VMEM(tuple(dims), BF),
        in_specs=[ANY] * len(arrays),
        out_specs=VM,
        scratch_shapes=[pltpu.SemaphoreType.DMA((len(arrays),))],
        compiler_params=pltpu.CompilerParams(vmem_limit_bytes=1 << 20),
        name=name,
    )(*pin(arrays))


def proj_kernel(spots, held, me_ref, fold_ref, *refs):
    piece_refs = refs[:spots]
    ld_ref = refs[spots]
    rows_ref, tag_ref = refs[spots + 1], refs[spots + 2]
    packs = refs[spots + 3 : spots + 5]
    all_ref, sems = refs[spots + 5 :]
    width = rows_ref.shape[0]
    group = piece_refs[0].shape[0]
    copies = [
        pltpu.make_async_copy(
            piece_refs[p], all_ref.at[pl.ds(p * group, group), :], sems.at[p]
        )
        for p in range(spots)
    ]
    for copy in copies:
        copy.start()
    for copy in copies:
        copy.wait()
    rows = all_ref[:, :width]
    rows_ref[...] = rows.T
    tags = all_ref[:, width:].astype(F32)
    tag_ref[...] = tags.T[0:8, :]
    labels = tags[:, 0:1]
    column = lax.broadcasted_iota(I32, (1, ld_ref.shape[1]), 1) // (2 * RANK)
    mine = me_ref[0] * held
    other = (me_ref[0] ^ 1) * held - held
    holder = jnp.where(column < held, column + mine, column + other).astype(F32)
    prod = jnp.dot(rows, ld_ref[...], preferred_element_type=F32)
    kept = jnp.where(labels == holder, prod, 0.0).astype(BF)
    folded = jnp.dot(kept, fold_ref[...], preferred_element_type=F32)
    lanes = packs[0].shape[1]
    spot = lax.broadcasted_iota(I32, (1, lanes), 1) // (2 * RANK)
    for s in range(2):
        total = jnp.zeros((group, lanes), F32)
        for p in range(spots):
            total = total + jnp.where(
                spot == (p ^ s), folded[p * group : (p + 1) * group, :], 0.0
            )
        packs[s][...] = total.astype(BF)


def nt(a, b):
    return lax.dot_general(a, b, (((1,), (1,)), ((), ())), preferred_element_type=F32)


def main_kernel(side, rows_ref, w_ref, raw_ref):
    for g in range(2):
        raw_ref[g, :, :] = jnp.dot(
            w_ref[2 * side + g, :, :], rows_ref[...], preferred_element_type=F32
        )


def mix_kernel(mask, own_ref, got_ref, sum_ref, out_ref):
    total = own_ref[...].astype(F32) + got_ref[...].astype(F32)
    sum_ref[...] = total.astype(BF)
    lanes = total.shape[1]
    step = mask * 2 * RANK
    spot = lax.broadcasted_iota(I32, total.shape, 1) // (2 * RANK)
    up = pltpu.roll(total, step, 1)
    down = pltpu.roll(total, lanes - step, 1)
    out_ref[...] = jnp.where(spot & mask == 0, down, up).astype(BF)


def down_kernel(spots, tile_ref, *refs):
    own_ref, got_ref, tag_ref = refs[:3]
    raw_refs, (lu_ref, dn_ref), outs = refs[3:5], refs[5:7], refs[7:]
    lanes = own_ref.shape[1]
    low = own_ref[...].astype(F32) + got_ref[...].astype(F32)
    spot = lax.broadcasted_iota(I32, (1, lanes), 1) // (2 * RANK)
    low = jnp.concatenate(
        [jnp.where(spot == p, low, 0.0).astype(BF) for p in range(spots)], axis=0
    )
    labels = tag_ref[0:1, :]
    wide = tile_ref.shape[1]
    owner = (lax.broadcasted_iota(I32, (wide, 1), 0) // RANK).astype(F32)
    mark = labels == owner
    spread = [jnp.where(mark, nt(tile_ref[g, :, :], low), 0.0).astype(BF) for g in range(2)]
    hidden = []
    for side in range(2):
        act = [
            raw_refs[side][g, :, :]
            + jnp.dot(lu_ref[2 * side + g, :, :], spread[g], preferred_element_type=F32)
            for g in range(2)
        ]
        hidden.append((act[0] / (1.0 + jnp.exp(-act[0])) * act[1]).astype(BF))
    total = lax.dot_general(
        jnp.concatenate(hidden, axis=0),
        dn_ref[...],
        (((0,), (0,)), ((), ())),
        preferred_element_type=F32,
    )
    start = 0
    for ref in outs:
        ref[...] = total[start : start + ref.shape[0], :].astype(BF)
        start += ref.shape[0]


def add_kernel(a_ref, b_ref, o_ref):
    o_ref[...] = (a_ref[...].astype(F32) + b_ref[...].astype(F32)).astype(BF)


def sum_kernel(*refs):
    size = refs[0].shape[0]
    total = refs[0][...].astype(F32)
    for ref in refs[1:-1]:
        total = total + ref[:size, :].astype(F32)
    refs[-1][...] = total.astype(BF)


def back_kernel(experts, capacity, z_ref, ids_ref, idc_ref, gw_ref, tok_ref, *refs):
    backs = refs[:-1]
    out_ref = refs[-1]
    local_tokens = tok_ref.shape[0]
    puts = one_hots(ids_ref, z_ref[0], experts, capacity, local_tokens)
    total = None
    for d in range(experts):
        scale = jnp.sum(
            jnp.where(idc_ref[...] == (z_ref[0] ^ d), gw_ref[...], 0.0), axis=1, keepdims=True
        )
        got = lax.dot_general(
            puts[d].astype(BF),
            backs[d][...],
            (((0,), (0,)), ((), ())),
            preferred_element_type=F32,
        )
        total = scale * got if total is None else total + scale * got
    out_ref[...] = (tok_ref[...].astype(F32) + total).astype(BF)


def after(values, deps):
    return lax.optimization_barrier((values, deps))[0]


def gather_first(own, bits):
    out = {0: own}
    for j in range(len(bits)):
        out[1 << j] = hop(own, 1 << j, bits)
    return out


def gather_second(have, bits):
    out = dict(have)
    for j in range(1, len(bits)):
        for p in range(1, 1 << j):
            out[p | 1 << j] = hop(out[p], 1 << j, bits)
    return [out[p] for p in range(1 << len(bits))]


def reduce_first(parts, bits, wait=()):
    table, gots = list(parts), []
    for j in reversed(range(1, len(bits))):
        for q in reversed(range(1 << j)):
            got = hop(table[q | 1 << j], 1 << j, bits)
            if q:
                table[q] = call(
                    add_kernel, [shape(*got.shape)], (after(table[q], wait), got), [VM] * 2, got.size, "add_rows"
                )[0]
            else:
                gots.append(got)
    return table[0], table[1], gots


def reduce_second(state, bits):
    own, last, gots = state
    return call(
        sum_kernel,
        [shape(*own.shape)],
        (own, *gots, hop(last, 1, bits)),
        [VM] * (2 + len(gots)),
        own.size,
        "sum_rows",
    )[0]


def body(
    tokens,
    expert_ids,
    gate_weights,
    request_lengths,
    request_adapter,
    expert_weights,
    expert_down,
    low_down,
    low_up,
):
    experts = lax.axis_size("expert")
    n_dp = lax.axis_size("dp")
    local_tokens, width = tokens.shape
    capacity = local_tokens * TOP * 4 // (3 * experts)
    held = low_down.shape[2] // (2 * RANK)
    adapters = low_up.shape[2] // RANK
    units = expert_down.shape[1]
    bits = []
    b = 2
    while b < n_dp:
        bits.append(b)
        b *= 2
    spots = 1 << len(bits)
    z = lax.axis_index("expert").astype(I32).reshape(1)
    me = lax.axis_index("dp").astype(I32).reshape(1)
    ids_t = expert_ids.T

    outgoing = call(
        functools.partial(front_kernel, experts, capacity),
        [pltpu.HBM((capacity, width + LANES), BF)] * experts,
        (z, *pin([request_lengths, request_adapter, ids_t, tokens])),
        [SM, ANY, ANY, ANY, ANY],
        2 * experts * capacity * local_tokens * width,
        "front",
        [
            pltpu.SMEM(request_lengths.shape, I32),
            pltpu.SMEM(request_adapter.shape, I32),
            pltpu.VMEM(ids_t.shape, I32),
            pltpu.VMEM(tokens.shape, BF),
            pltpu.VMEM((experts, capacity, width + LANES), BF),
            pltpu.SemaphoreType.DMA((4,)),
            pltpu.SemaphoreType.DMA((experts,)),
        ],
        ANY,
    )
    wt_t = jnp.swapaxes(expert_weights[0], 1, 2)
    lu_t = jnp.swapaxes(low_up[0], 1, 2)
    ld_o = swap(low_down[0], "dp", 1)
    wt_o = swap(after(wt_t, outgoing), "dp", 1)
    ld = stage([low_down[0], ld_o], 1, "stage_low_down")
    wt = stage([wt_t, wt_o], 0, "stage_gate_up")
    lanes = 2 * RANK * spots
    fold = (
        jnp.arange(4 * held * RANK)[:, None] % (2 * RANK) == jnp.arange(lanes)[None, :] % (2 * RANK)
    ).astype(BF)
    tile = jnp.stack(
        [
            (
                jnp.arange(lanes)[None, :] % (2 * RANK)
                == jnp.arange(adapters * RANK)[:, None] % RANK + g * RANK
            ).astype(BF)
            for g in range(2)
        ]
    )

    order = list(range(experts))
    first, second = {}, {}
    first[0] = gather_first(outgoing[0], bits)
    arrived = [outgoing[0]] + [swap(outgoing[order[i]], "expert", order[i]) for i in (1, 2)]

    group = capacity
    count = group * spots
    parts, done, adds = {}, {}, {}
    first[0] = after(first[0], (arrived[1], ld_o))
    second[0] = gather_second(first[0], bits)
    lu_o = swap(after(lu_t, (wt_o, first[0])), "dp", 1)
    dn_o = swap(after(expert_down[0], (lu_o, second[0])), "dp", 1)
    lu = stage([lu_t, lu_o], 0, "stage_low_up")
    dn = stage([expert_down[0], dn_o], 0, "stage_down")
    first[1] = gather_first(after(arrived[1], second[0]), bits)
    last = experts - 1
    backs = [None] * experts

    def give(j):
        backs[order[j]] = done[j] if order[j] == 0 else swap(done[j], "expert", order[j])

    for i, d in enumerate(order):
        deps = [first[2]] if i == 1 else [wt] if i == 0 else []
        if i >= 1:
            deps.append(parts[i - 1][0])
        if i >= 2:
            done[i - 2] = reduce_second(adds[i - 2], bits)
            deps.append(done[i - 2])
            give(i - 2)
        pieces = after(second[i], deps)
        got = call(
            functools.partial(proj_kernel, spots, held),
            [shape(width, count), shape(8, count, F32)] + [shape(group, lanes)] * 2,
            (me, fold, *pin(pieces), ld),
            [SM, VM] + [ANY] * spots + [VM],
            4 * count * width * held * 2 * RANK,
            "project",
            [pltpu.VMEM((count, width + LANES), BF), pltpu.SemaphoreType.DMA((spots,))],
        )
        rows, tags, low, send = got
        deps = [first[1]] if i == 0 else [second[3]] if i == 2 else []
        if i == 0:
            second[1] = gather_second(after(first[1], low), bits)
            first[2] = gather_first(after(arrived[2], low), bits)
            second[2] = gather_second(first[2], bits)
        rows = after(rows, deps)
        raw = []
        for side in range(2):
            raw.append(
                call(
                    functools.partial(main_kernel, side),
                    [jax.ShapeDtypeStruct((2, units, count), F32)],
                    (rows, wt),
                    [VM] * 2,
                    4 * count * width * units,
                    "gate_up",
                )[0]
            )
            if side == 0:
                recv = hop(send, 1, bits)
                early = raw[0]
                low = after(low, early)
                if i >= 1:
                    adds[i - 1] = reduce_first(parts[i - 1], bits, raw)
                    low = after(low, adds[i - 1][1])
                for j in range(1, len(bits)):
                    low, send = call(
                        functools.partial(mix_kernel, 1 << j),
                        [shape(group, lanes)] * 2,
                        (low, recv),
                        [VM] * 2,
                        group * lanes,
                        "mix",
                    )
                    recv = hop(send, 1 << j, bits)
                rows = after(rows, low)
        if i == 0:
            for j in range(3, experts):
                piece = after(outgoing[order[j]], (arrived[j - 1], early))
                arrived.append(swap(piece, "expert", order[j]))
                first[j] = gather_first(after(arrived[j], raw), bits)
                second[j] = gather_second(first[j], bits)
        deps = [second[1]] if i == 0 else [second[2], first[3]] if i == 1 else []
        raw = after(raw, deps)
        parts[i] = call(
            functools.partial(down_kernel, spots),
            [shape(group, width)] * spots,
            (tile, low, recv, tags, *raw, lu, dn),
            [VM] * 8,
            8 * count * adapters * RANK * units + 4 * count * units * width,
            "down",
        )
    done[last - 1] = reduce_second(adds[last - 1], bits)
    give(last - 1)
    own, left, gots = reduce_first(parts[last], bits)
    own = after(own, [backs[order[i]] for i in range(last)])
    done[last] = reduce_second((own, left, gots), bits)
    give(last)

    return call(
        functools.partial(back_kernel, experts, capacity),
        [shape(local_tokens, width)],
        (z, ids_t, expert_ids, gate_weights, tokens, *backs),
        [SM] + [VM] * (4 + experts),
        2 * experts * capacity * local_tokens * width,
        "combine",
    )[0]


def solution(mesh):
    return jax.shard_map(
        body,
        mesh=mesh,
        in_specs=(
            P(("expert", "dp"), None),
            P(("expert", "dp"), None),
            P(("expert", "dp"), None),
            P(("expert", "dp"), None),
            P(("expert", "dp"), None),
            P("expert", None, None, "dp"),
            P("expert", "dp", None),
            P("expert", None, "dp"),
            P("expert", None, None, "dp"),
        ),
        out_specs=P(("expert", "dp"), None),
        check_vma=False,
    )
```

```python
import functools

import jax
import jax.numpy as jnp
from jax import lax
from jax.experimental import pallas as pl
from jax.experimental.pallas import tpu as pltpu
from jax.sharding import PartitionSpec as P

TOP = 2
RANK = 16
LANES = 128
COST = 16
BF = jnp.bfloat16
F32 = jnp.float32
I32 = jnp.int32
VM = pl.BlockSpec(memory_space=pltpu.VMEM)
SM = pl.BlockSpec(memory_space=pltpu.SMEM)
ANY = pl.BlockSpec(memory_space=pltpu.HBM)


def swap(x, axis, bit):
    n = lax.axis_size(axis)
    return lax.ppermute(x, axis, [(i, i ^ bit) for i in range(n)])


def spot_mask(index, spot, bits):
    turn = index & 1 if len(bits) == 2 else 0
    mask = 0
    for j in range(len(bits)):
        if spot >> j & 1:
            mask ^= bits[j ^ turn]
    return mask


def hop(x, spot, bits):
    n = lax.axis_size("dp")
    return lax.ppermute(x, "dp", [(i, i ^ spot_mask(i, spot, bits)) for i in range(n)])


def call(fn, outs, args, specs, flops, name, scratch=(), out_spec=VM):
    size = sum(a.size * a.dtype.itemsize for a in args)
    return pl.pallas_call(
        fn,
        out_shape=tuple(outs),
        in_specs=specs,
        out_specs=tuple(out_spec for _ in outs),
        scratch_shapes=scratch,
        compiler_params=pltpu.CompilerParams(vmem_limit_bytes=16 << 20),
        cost_estimate=pl.CostEstimate(
            flops=flops // COST, bytes_accessed=size // COST, transcendentals=0
        ),
        name=name,
    )(*args)


def pin(arrays):
    return [pltpu.with_memory_space_constraint(a, pltpu.HBM) for a in arrays]


def shape(rows, cols, dtype=BF):
    return jax.ShapeDtypeStruct((rows, cols), dtype)


def one_hots(ids_ref, z, experts, capacity, local_tokens):
    first = ids_ref[0:1, :]
    second = ids_ref[1:2, :]
    member = jnp.concatenate(
        [((first == (z ^ d)) | (second == (z ^ d))).astype(F32) for d in range(experts)], axis=0
    )
    before = (
        lax.broadcasted_iota(I32, (local_tokens, local_tokens), 0)
        < lax.broadcasted_iota(I32, (local_tokens, local_tokens), 1)
    ).astype(F32)
    slot = jnp.dot(member.astype(BF), before.astype(BF), preferred_element_type=F32)
    rank = lax.broadcasted_iota(I32, (capacity, local_tokens), 0).astype(F32)
    return [
        jnp.where((rank == slot[d : d + 1, :]) & (member[d : d + 1, :] > 0.0), 1.0, 0.0)
        for d in range(experts)
    ]


def front_kernel(experts, capacity, z_ref, len_hbm, ada_hbm, ids_hbm, tok_hbm, *refs):
    outs = refs[:experts]
    len_ref, ada_ref, ids_ref, tok_ref, put_ref, sems, out_sems = refs[experts:]
    copies = [
        pltpu.make_async_copy(src, dst, sems.at[i])
        for i, (src, dst) in enumerate(
            [(tok_hbm, tok_ref), (ids_hbm, ids_ref), (len_hbm, len_ref), (ada_hbm, ada_ref)]
        )
    ]
    for copy in copies:
        copy.start()
    for copy in copies:
        copy.wait()
    local_tokens, width = tok_ref.shape
    values = tok_ref[...].astype(F32)
    normed = (
        values * lax.rsqrt(jnp.mean(values * values, axis=1, keepdims=True) + 1e-05)
    ).astype(BF)
    place = lax.broadcasted_iota(I32, (local_tokens, LANES), 0)
    lane = lax.broadcasted_iota(I32, (local_tokens, LANES), 1)
    tag = jnp.zeros((local_tokens, LANES), F32) + ada_ref[0, 0].astype(F32)
    end = len_ref[0, 0]
    for r in range(1, len_ref.shape[1]):
        tag = jnp.where(place >= end, ada_ref[0, r].astype(F32), tag)
        end = end + len_ref[0, r]
    tag = jnp.where(lane == 0, tag, 0.0).astype(BF)
    puts = one_hots(ids_ref, z_ref[0], experts, capacity, local_tokens)
    sends = []
    for d in range(experts):
        put = puts[d].astype(BF)
        put_ref[d, :, :width] = jnp.dot(put, normed, preferred_element_type=F32).astype(BF)
        put_ref[d, :, width:] = jnp.dot(put, tag, preferred_element_type=F32).astype(BF)
        sends.append(pltpu.make_async_copy(put_ref.at[d], outs[d], out_sems.at[d]))
        sends[d].start()
    for send in sends:
        send.wait()


def stage_kernel(axis, *refs):
    out_ref, sems = refs[-2:]
    copies = []
    start = 0
    for i, ref in enumerate(refs[:-2]):
        size = ref.shape[axis]
        where = tuple([slice(None)] * axis + [pl.ds(start, size)])
        copies.append(pltpu.make_async_copy(ref, out_ref.at[where], sems.at[i]))
        start += size
    for copy in copies:
        copy.start()
    for copy in copies:
        copy.wait()


def stage(arrays, axis, name):
    dims = list(arrays[0].shape)
    dims[axis] = sum(a.shape[axis] for a in arrays)
    return pl.pallas_call(
        functools.partial(stage_kernel, axis),
        out_shape=pltpu.VMEM(tuple(dims), BF),
        in_specs=[ANY] * len(arrays),
        out_specs=VM,
        scratch_shapes=[pltpu.SemaphoreType.DMA((len(arrays),))],
        compiler_params=pltpu.CompilerParams(vmem_limit_bytes=1 << 20),
        name=name,
    )(*pin(arrays))


def proj_kernel(spots, held, me_ref, fold_ref, *refs):
    piece_refs = refs[:spots]
    ld_ref = refs[spots]
    rows_ref, tag_ref = refs[spots + 1], refs[spots + 2]
    packs = refs[spots + 3 : spots + 5]
    all_ref, sems = refs[spots + 5 :]
    width = rows_ref.shape[0]
    group = piece_refs[0].shape[0]
    copies = [
        pltpu.make_async_copy(
            piece_refs[p], all_ref.at[pl.ds(p * group, group), :], sems.at[p]
        )
        for p in range(spots)
    ]
    for copy in copies:
        copy.start()
    for copy in copies:
        copy.wait()
    rows = all_ref[:, :width]
    rows_ref[...] = rows.T
    tags = all_ref[:, width:].astype(F32)
    tag_ref[...] = tags.T[0:8, :]
    labels = tags[:, 0:1]
    column = lax.broadcasted_iota(I32, (1, ld_ref.shape[1]), 1) // (2 * RANK)
    mine = me_ref[0] * held
    other = (me_ref[0] ^ 1) * held - held
    holder = jnp.where(column < held, column + mine, column + other).astype(F32)
    prod = jnp.dot(rows, ld_ref[...], preferred_element_type=F32)
    kept = jnp.where(labels == holder, prod, 0.0).astype(BF)
    folded = jnp.dot(kept, fold_ref[...], preferred_element_type=F32)
    lanes = packs[0].shape[1]
    spot = lax.broadcasted_iota(I32, (1, lanes), 1) // (2 * RANK)
    for s in range(2):
        total = jnp.zeros((group, lanes), F32)
        for p in range(spots):
            total = total + jnp.where(
                spot == (p ^ s), folded[p * group : (p + 1) * group, :], 0.0
            )
        packs[s][...] = total.astype(BF)


def nt(a, b):
    return lax.dot_general(a, b, (((1,), (1,)), ((), ())), preferred_element_type=F32)


def main_kernel(side, rows_ref, w_ref, raw_ref):
    for g in range(2):
        raw_ref[g, :, :] = jnp.dot(
            w_ref[2 * side + g, :, :], rows_ref[...], preferred_element_type=F32
        )


def mix_kernel(mask, own_ref, got_ref, sum_ref, out_ref):
    total = own_ref[...].astype(F32) + got_ref[...].astype(F32)
    sum_ref[...] = total.astype(BF)
    lanes = total.shape[1]
    step = mask * 2 * RANK
    spot = lax.broadcasted_iota(I32, total.shape, 1) // (2 * RANK)
    up = pltpu.roll(total, step, 1)
    down = pltpu.roll(total, lanes - step, 1)
    out_ref[...] = jnp.where(spot & mask == 0, down, up).astype(BF)


def down_kernel(spots, tile_ref, *refs):
    own_ref, got_ref, tag_ref = refs[:3]
    raw_refs, (lu_ref, dn_ref), outs = refs[3:5], refs[5:7], refs[7:]
    lanes = own_ref.shape[1]
    low = own_ref[...].astype(F32) + got_ref[...].astype(F32)
    spot = lax.broadcasted_iota(I32, (1, lanes), 1) // (2 * RANK)
    low = jnp.concatenate(
        [jnp.where(spot == p, low, 0.0).astype(BF) for p in range(spots)], axis=0
    )
    labels = tag_ref[0:1, :]
    wide = tile_ref.shape[1]
    owner = (lax.broadcasted_iota(I32, (wide, 1), 0) // RANK).astype(F32)
    mark = labels == owner
    spread = [jnp.where(mark, nt(tile_ref[g, :, :], low), 0.0).astype(BF) for g in range(2)]
    hidden = []
    for side in range(2):
        act = [
            raw_refs[side][g, :, :]
            + jnp.dot(lu_ref[2 * side + g, :, :], spread[g], preferred_element_type=F32)
            for g in range(2)
        ]
        hidden.append((act[0] / (1.0 + jnp.exp(-act[0])) * act[1]).astype(BF))
    total = lax.dot_general(
        jnp.concatenate(hidden, axis=0),
        dn_ref[...],
        (((0,), (0,)), ((), ())),
        preferred_element_type=F32,
    )
    start = 0
    for ref in outs:
        ref[...] = total[start : start + ref.shape[0], :].astype(BF)
        start += ref.shape[0]


def add_kernel(a_ref, b_ref, o_ref):
    o_ref[...] = (a_ref[...].astype(F32) + b_ref[...].astype(F32)).astype(BF)


def sum_kernel(*refs):
    size = refs[0].shape[0]
    total = refs[0][...].astype(F32)
    for ref in refs[1:-1]:
        total = total + ref[:size, :].astype(F32)
    refs[-1][...] = total.astype(BF)


def back_kernel(experts, capacity, z_ref, ids_ref, idc_ref, gw_ref, tok_ref, *refs):
    backs = refs[:-1]
    out_ref = refs[-1]
    local_tokens = tok_ref.shape[0]
    puts = one_hots(ids_ref, z_ref[0], experts, capacity, local_tokens)
    total = None
    for d in range(experts):
        scale = jnp.sum(
            jnp.where(idc_ref[...] == (z_ref[0] ^ d), gw_ref[...], 0.0), axis=1, keepdims=True
        )
        got = lax.dot_general(
            puts[d].astype(BF),
            backs[d][...],
            (((0,), (0,)), ((), ())),
            preferred_element_type=F32,
        )
        total = scale * got if total is None else total + scale * got
    out_ref[...] = (tok_ref[...].astype(F32) + total).astype(BF)


def after(values, deps):
    return lax.optimization_barrier((values, deps))[0]


def gather_first(own, bits):
    out = {0: own}
    for j in range(len(bits)):
        out[1 << j] = hop(own, 1 << j, bits)
    return out


def gather_second(have, bits):
    out = dict(have)
    for j in range(1, len(bits)):
        for p in range(1, 1 << j):
            out[p | 1 << j] = hop(out[p], 1 << j, bits)
    return [out[p] for p in range(1 << len(bits))]


def reduce_first(parts, bits, wait=()):
    table, gots = list(parts), []
    for j in reversed(range(1, len(bits))):
        for q in reversed(range(1 << j)):
            got = hop(table[q | 1 << j], 1 << j, bits)
            if q:
                table[q] = call(
                    add_kernel, [shape(*got.shape)], (after(table[q], wait), got), [VM] * 2, got.size, "add_rows"
                )[0]
            else:
                gots.append(got)
    return table[0], table[1], gots


def reduce_second(state, bits):
    own, last, gots = state
    return call(
        sum_kernel,
        [shape(*own.shape)],
        (own, *gots, hop(last, 1, bits)),
        [VM] * (2 + len(gots)),
        own.size,
        "sum_rows",
    )[0]


def body(
    tokens,
    expert_ids,
    gate_weights,
    request_lengths,
    request_adapter,
    expert_weights,
    expert_down,
    low_down,
    low_up,
):
    experts = lax.axis_size("expert")
    n_dp = lax.axis_size("dp")
    local_tokens, width = tokens.shape
    capacity = local_tokens * TOP * 4 // (3 * experts)
    held = low_down.shape[2] // (2 * RANK)
    adapters = low_up.shape[2] // RANK
    units = expert_down.shape[1]
    bits = []
    b = 2
    while b < n_dp:
        bits.append(b)
        b *= 2
    spots = 1 << len(bits)
    z = lax.axis_index("expert").astype(I32).reshape(1)
    me = lax.axis_index("dp").astype(I32).reshape(1)
    ids_t = expert_ids.T

    outgoing = call(
        functools.partial(front_kernel, experts, capacity),
        [pltpu.HBM((capacity, width + LANES), BF)] * experts,
        (z, *pin([request_lengths, request_adapter, ids_t, tokens])),
        [SM, ANY, ANY, ANY, ANY],
        2 * experts * capacity * local_tokens * width,
        "front",
        [
            pltpu.SMEM(request_lengths.shape, I32),
            pltpu.SMEM(request_adapter.shape, I32),
            pltpu.VMEM(ids_t.shape, I32),
            pltpu.VMEM(tokens.shape, BF),
            pltpu.VMEM((experts, capacity, width + LANES), BF),
            pltpu.SemaphoreType.DMA((4,)),
            pltpu.SemaphoreType.DMA((experts,)),
        ],
        ANY,
    )
    wt_t = jnp.swapaxes(expert_weights[0], 1, 2)
    lu_t = jnp.swapaxes(low_up[0], 1, 2)
    ld_o = swap(low_down[0], "dp", 1)
    wt_o = swap(after(wt_t, outgoing), "dp", 1)
    ld = stage([low_down[0], ld_o], 1, "stage_low_down")
    wt = stage([wt_t, wt_o], 0, "stage_gate_up")
    lanes = 2 * RANK * spots
    fold = (
        jnp.arange(4 * held * RANK)[:, None] % (2 * RANK) == jnp.arange(lanes)[None, :] % (2 * RANK)
    ).astype(BF)
    tile = jnp.stack(
        [
            (
                jnp.arange(lanes)[None, :] % (2 * RANK)
                == jnp.arange(adapters * RANK)[:, None] % RANK + g * RANK
            ).astype(BF)
            for g in range(2)
        ]
    )

    order = list(range(experts))
    first, second = {}, {}
    first[0] = gather_first(outgoing[0], bits)
    arrived = [outgoing[0]] + [swap(outgoing[order[i]], "expert", order[i]) for i in (1, 2)]

    group = capacity
    count = group * spots
    parts, done, adds = {}, {}, {}
    first[0] = after(first[0], (arrived[1], ld_o))
    second[0] = gather_second(first[0], bits)
    lu_o = swap(after(lu_t, (wt_o, first[0])), "dp", 1)
    dn_o = swap(after(expert_down[0], (lu_o, second[0])), "dp", 1)
    lu = stage([lu_t, lu_o], 0, "stage_low_up")
    dn = stage([expert_down[0], dn_o], 0, "stage_down")
    first[1] = gather_first(after(arrived[1], (second[0], wt, ld)), bits)
    last = experts - 1
    backs = [None] * experts

    def give(j):
        backs[order[j]] = done[j] if order[j] == 0 else swap(done[j], "expert", order[j])

    for i, d in enumerate(order):
        deps = [first[2]] if i == 1 else [wt] if i == 0 else []
        if i >= 1:
            deps.append(parts[i - 1][0])
        if i >= 2:
            done[i - 2] = reduce_second(adds[i - 2], bits)
            deps.append(done[i - 2])
            give(i - 2)
        pieces = after(second[i], deps)
        got = call(
            functools.partial(proj_kernel, spots, held),
            [shape(width, count), shape(8, count, F32)] + [shape(group, lanes)] * 2,
            (me, fold, *pin(pieces), ld),
            [SM, VM] + [ANY] * spots + [VM],
            4 * count * width * held * 2 * RANK,
            "project",
            [pltpu.VMEM((count, width + LANES), BF), pltpu.SemaphoreType.DMA((spots,))],
        )
        rows, tags, low, send = got
        deps = [first[1], dn_o] if i == 0 else [second[3]] if i == 2 else []
        if i == 0:
            second[1] = gather_second(after(first[1], low), bits)
            first[2] = gather_first(after(arrived[2], low), bits)
            second[2] = gather_second(first[2], bits)
        rows = after(rows, deps)
        raw = []
        for side in range(2):
            raw.append(
                call(
                    functools.partial(main_kernel, side),
                    [jax.ShapeDtypeStruct((2, units, count), F32)],
                    (rows, wt),
                    [VM] * 2,
                    4 * count * width * units,
                    "gate_up",
                )[0]
            )
            if side == 0:
                recv = hop(send, 1, bits)
                early = raw[0]
                low = after(low, early)
                if i >= 1:
                    adds[i - 1] = reduce_first(parts[i - 1], bits, raw)
                    low = after(low, adds[i - 1][1])
                for j in range(1, len(bits)):
                    low, send = call(
                        functools.partial(mix_kernel, 1 << j),
                        [shape(group, lanes)] * 2,
                        (low, recv),
                        [VM] * 2,
                        group * lanes,
                        "mix",
                    )
                    recv = hop(send, 1 << j, bits)
                rows = after(rows, low)
        if i == 0:
            for j in range(3, experts):
                piece = after(outgoing[order[j]], (arrived[j - 1], early))
                arrived.append(swap(piece, "expert", order[j]))
                first[j] = gather_first(after(arrived[j], raw), bits)
                second[j] = gather_second(first[j], bits)
        deps = [second[1]] if i == 0 else [second[2], first[3]] if i == 1 else []
        raw = after(raw, deps)
        parts[i] = call(
            functools.partial(down_kernel, spots),
            [shape(group, width)] * spots,
            (tile, low, recv, tags, *raw, lu, dn),
            [VM] * 8,
            8 * count * adapters * RANK * units + 4 * count * units * width,
            "down",
        )
    done[last - 1] = reduce_second(adds[last - 1], bits)
    give(last - 1)
    own, left, gots = reduce_first(parts[last], bits)
    own = after(own, [backs[order[i]] for i in range(last)])
    done[last] = reduce_second((own, left, gots), bits)
    give(last)

    return call(
        functools.partial(back_kernel, experts, capacity),
        [shape(local_tokens, width)],
        (z, ids_t, expert_ids, gate_weights, tokens, *backs),
        [SM] + [VM] * (4 + experts),
        2 * experts * capacity * local_tokens * width,
        "combine",
    )[0]


def solution(mesh):
    return jax.shard_map(
        body,
        mesh=mesh,
        in_specs=(
            P(("expert", "dp"), None),
            P(("expert", "dp"), None),
            P(("expert", "dp"), None),
            P(("expert", "dp"), None),
            P(("expert", "dp"), None),
            P("expert", None, None, "dp"),
            P("expert", "dp", None),
            P("expert", None, "dp"),
            P("expert", None, None, "dp"),
        ),
        out_specs=P(("expert", "dp"), None),
        check_vma=False,
    )
```

```python
import functools

import jax
import jax.numpy as jnp
from jax import lax
from jax.experimental import pallas as pl
from jax.experimental.pallas import tpu as pltpu
from jax.sharding import PartitionSpec as P

TOP = 2
RANK = 16
LANES = 128
COST = 16
BF = jnp.bfloat16
F32 = jnp.float32
I32 = jnp.int32
VM = pl.BlockSpec(memory_space=pltpu.VMEM)
SM = pl.BlockSpec(memory_space=pltpu.SMEM)
ANY = pl.BlockSpec(memory_space=pltpu.HBM)


def swap(x, axis, bit):
    n = lax.axis_size(axis)
    return lax.ppermute(x, axis, [(i, i ^ bit) for i in range(n)])


def spot_mask(index, spot, bits):
    turn = index & 1 if len(bits) == 2 else 0
    mask = 0
    for j in range(len(bits)):
        if spot >> j & 1:
            mask ^= bits[j ^ turn]
    return mask


def hop(x, spot, bits):
    n = lax.axis_size("dp")
    return lax.ppermute(x, "dp", [(i, i ^ spot_mask(i, spot, bits)) for i in range(n)])


def call(fn, outs, args, specs, flops, name, scratch=(), out_spec=VM):
    size = sum(a.size * a.dtype.itemsize for a in args)
    return pl.pallas_call(
        fn,
        out_shape=tuple(outs),
        in_specs=specs,
        out_specs=tuple(out_spec for _ in outs),
        scratch_shapes=scratch,
        compiler_params=pltpu.CompilerParams(vmem_limit_bytes=16 << 20),
        cost_estimate=pl.CostEstimate(
            flops=flops // COST, bytes_accessed=size // COST, transcendentals=0
        ),
        name=name,
    )(*args)


def pin(arrays):
    return [pltpu.with_memory_space_constraint(a, pltpu.HBM) for a in arrays]


def shape(rows, cols, dtype=BF):
    return jax.ShapeDtypeStruct((rows, cols), dtype)


def one_hots(ids_ref, z, experts, capacity, local_tokens):
    first = ids_ref[0:1, :]
    second = ids_ref[1:2, :]
    member = jnp.concatenate(
        [((first == (z ^ d)) | (second == (z ^ d))).astype(F32) for d in range(experts)], axis=0
    )
    before = (
        lax.broadcasted_iota(I32, (local_tokens, local_tokens), 0)
        < lax.broadcasted_iota(I32, (local_tokens, local_tokens), 1)
    ).astype(F32)
    slot = jnp.dot(member.astype(BF), before.astype(BF), preferred_element_type=F32)
    rank = lax.broadcasted_iota(I32, (capacity, local_tokens), 0).astype(F32)
    return [
        jnp.where((rank == slot[d : d + 1, :]) & (member[d : d + 1, :] > 0.0), 1.0, 0.0)
        for d in range(experts)
    ]


def front_kernel(experts, capacity, z_ref, len_hbm, ada_hbm, ids_hbm, tok_hbm, *refs):
    outs = refs[:experts]
    len_ref, ada_ref, ids_ref, tok_ref, put_ref, sems, out_sems = refs[experts:]
    copies = [
        pltpu.make_async_copy(src, dst, sems.at[i])
        for i, (src, dst) in enumerate(
            [(tok_hbm, tok_ref), (ids_hbm, ids_ref), (len_hbm, len_ref), (ada_hbm, ada_ref)]
        )
    ]
    for copy in copies:
        copy.start()
    for copy in copies:
        copy.wait()
    local_tokens, width = tok_ref.shape
    values = tok_ref[...].astype(F32)
    normed = (
        values * lax.rsqrt(jnp.mean(values * values, axis=1, keepdims=True) + 1e-05)
    ).astype(BF)
    place = lax.broadcasted_iota(I32, (local_tokens, LANES), 0)
    lane = lax.broadcasted_iota(I32, (local_tokens, LANES), 1)
    tag = jnp.zeros((local_tokens, LANES), F32) + ada_ref[0, 0].astype(F32)
    end = len_ref[0, 0]
    for r in range(1, len_ref.shape[1]):
        tag = jnp.where(place >= end, ada_ref[0, r].astype(F32), tag)
        end = end + len_ref[0, r]
    tag = jnp.where(lane == 0, tag, 0.0).astype(BF)
    puts = one_hots(ids_ref, z_ref[0], experts, capacity, local_tokens)
    sends = []
    for d in range(experts):
        put = puts[d].astype(BF)
        put_ref[d, :, :width] = jnp.dot(put, normed, preferred_element_type=F32).astype(BF)
        put_ref[d, :, width:] = jnp.dot(put, tag, preferred_element_type=F32).astype(BF)
        sends.append(pltpu.make_async_copy(put_ref.at[d], outs[d], out_sems.at[d]))
        sends[d].start()
    for send in sends:
        send.wait()


def stage_kernel(axis, *refs):
    out_ref, sems = refs[-2:]
    copies = []
    start = 0
    for i, ref in enumerate(refs[:-2]):
        size = ref.shape[axis]
        where = tuple([slice(None)] * axis + [pl.ds(start, size)])
        copies.append(pltpu.make_async_copy(ref, out_ref.at[where], sems.at[i]))
        start += size
    for copy in copies:
        copy.start()
    for copy in copies:
        copy.wait()


def stage(arrays, axis, name):
    dims = list(arrays[0].shape)
    dims[axis] = sum(a.shape[axis] for a in arrays)
    return pl.pallas_call(
        functools.partial(stage_kernel, axis),
        out_shape=pltpu.VMEM(tuple(dims), BF),
        in_specs=[ANY] * len(arrays),
        out_specs=VM,
        scratch_shapes=[pltpu.SemaphoreType.DMA((len(arrays),))],
        compiler_params=pltpu.CompilerParams(vmem_limit_bytes=1 << 20),
        name=name,
    )(*pin(arrays))


def proj_kernel(spots, held, me_ref, fold_ref, *refs):
    piece_refs = refs[:spots]
    ld_ref = refs[spots]
    rows_ref, tag_ref = refs[spots + 1], refs[spots + 2]
    packs = refs[spots + 3 : spots + 5]
    all_ref, sems = refs[spots + 5 :]
    width = rows_ref.shape[0]
    group = piece_refs[0].shape[0]
    copies = [
        pltpu.make_async_copy(
            piece_refs[p], all_ref.at[pl.ds(p * group, group), :], sems.at[p]
        )
        for p in range(spots)
    ]
    for copy in copies:
        copy.start()
    count = all_ref.shape[0]
    half = count // 2
    for part in range(2):
        for copy in copies[part * spots // 2 : (part + 1) * spots // 2]:
            copy.wait()
        span = slice(part * half, (part + 1) * half)
        rows_ref[:, span] = all_ref[span, :width].T
    rows = all_ref[:, :width]
    tags = all_ref[:, width:].astype(F32)
    tag_ref[...] = tags.T[0:8, :]
    labels = tags[:, 0:1]
    column = lax.broadcasted_iota(I32, (1, ld_ref.shape[1]), 1) // (2 * RANK)
    mine = me_ref[0] * held
    other = (me_ref[0] ^ 1) * held - held
    holder = jnp.where(column < held, column + mine, column + other).astype(F32)
    prod = jnp.dot(rows, ld_ref[...], preferred_element_type=F32)
    kept = jnp.where(labels == holder, prod, 0.0).astype(BF)
    folded = jnp.dot(kept, fold_ref[...], preferred_element_type=F32)
    lanes = packs[0].shape[1]
    spot = lax.broadcasted_iota(I32, (1, lanes), 1) // (2 * RANK)
    for s in range(2):
        total = jnp.zeros((group, lanes), F32)
        for p in range(spots):
            total = total + jnp.where(
                spot == (p ^ s), folded[p * group : (p + 1) * group, :], 0.0
            )
        packs[s][...] = total.astype(BF)


def nt(a, b):
    return lax.dot_general(a, b, (((1,), (1,)), ((), ())), preferred_element_type=F32)


def main_kernel(side, rows_ref, w_ref, raw_ref):
    for g in range(2):
        raw_ref[g, :, :] = jnp.dot(
            w_ref[2 * side + g, :, :], rows_ref[...], preferred_element_type=F32
        )


def mix_kernel(mask, own_ref, got_ref, sum_ref, out_ref):
    total = own_ref[...].astype(F32) + got_ref[...].astype(F32)
    sum_ref[...] = total.astype(BF)
    lanes = total.shape[1]
    step = mask * 2 * RANK
    spot = lax.broadcasted_iota(I32, total.shape, 1) // (2 * RANK)
    up = pltpu.roll(total, step, 1)
    down = pltpu.roll(total, lanes - step, 1)
    out_ref[...] = jnp.where(spot & mask == 0, down, up).astype(BF)


def down_kernel(spots, tile_ref, *refs):
    own_ref, got_ref, tag_ref = refs[:3]
    raw_refs, (lu_ref, dn_ref), outs = refs[3:5], refs[5:7], refs[7:]
    lanes = own_ref.shape[1]
    low = own_ref[...].astype(F32) + got_ref[...].astype(F32)
    spot = lax.broadcasted_iota(I32, (1, lanes), 1) // (2 * RANK)
    low = jnp.concatenate(
        [jnp.where(spot == p, low, 0.0).astype(BF) for p in range(spots)], axis=0
    )
    labels = tag_ref[0:1, :]
    wide = tile_ref.shape[1]
    owner = (lax.broadcasted_iota(I32, (wide, 1), 0) // RANK).astype(F32)
    mark = labels == owner
    spread = [jnp.where(mark, nt(tile_ref[g, :, :], low), 0.0).astype(BF) for g in range(2)]
    hidden = []
    for side in range(2):
        act = [
            raw_refs[side][g, :, :]
            + jnp.dot(lu_ref[2 * side + g, :, :], spread[g], preferred_element_type=F32)
            for g in range(2)
        ]
        hidden.append((act[0] / (1.0 + jnp.exp(-act[0])) * act[1]).astype(BF))
    total = lax.dot_general(
        jnp.concatenate(hidden, axis=0),
        dn_ref[...],
        (((0,), (0,)), ((), ())),
        preferred_element_type=F32,
    )
    start = 0
    for ref in outs:
        ref[...] = total[start : start + ref.shape[0], :].astype(BF)
        start += ref.shape[0]


def add_kernel(a_ref, b_ref, o_ref):
    o_ref[...] = (a_ref[...].astype(F32) + b_ref[...].astype(F32)).astype(BF)


def sum_kernel(*refs):
    size = refs[0].shape[0]
    total = refs[0][...].astype(F32)
    for ref in refs[1:-1]:
        total = total + ref[:size, :].astype(F32)
    refs[-1][...] = total.astype(BF)


def back_kernel(experts, capacity, z_ref, ids_ref, idc_ref, gw_ref, tok_ref, *refs):
    backs = refs[:-1]
    out_ref = refs[-1]
    local_tokens = tok_ref.shape[0]
    puts = one_hots(ids_ref, z_ref[0], experts, capacity, local_tokens)
    total = None
    for d in range(experts):
        scale = jnp.sum(
            jnp.where(idc_ref[...] == (z_ref[0] ^ d), gw_ref[...], 0.0), axis=1, keepdims=True
        )
        got = lax.dot_general(
            puts[d].astype(BF),
            backs[d][...],
            (((0,), (0,)), ((), ())),
            preferred_element_type=F32,
        )
        total = scale * got if total is None else total + scale * got
    out_ref[...] = (tok_ref[...].astype(F32) + total).astype(BF)


def after(values, deps):
    return lax.optimization_barrier((values, deps))[0]


def gather_first(own, bits):
    out = {0: own}
    for j in range(len(bits)):
        out[1 << j] = hop(own, 1 << j, bits)
    return out


def gather_second(have, bits):
    out = dict(have)
    for j in range(1, len(bits)):
        for p in range(1, 1 << j):
            out[p | 1 << j] = hop(out[p], 1 << j, bits)
    return [out[p] for p in range(1 << len(bits))]


def reduce_first(parts, bits, wait=()):
    table, gots = list(parts), []
    for j in reversed(range(1, len(bits))):
        for q in reversed(range(1 << j)):
            got = hop(table[q | 1 << j], 1 << j, bits)
            if q:
                table[q] = call(
                    add_kernel, [shape(*got.shape)], (after(table[q], wait), got), [VM] * 2, got.size, "add_rows"
                )[0]
            else:
                gots.append(got)
    return table[0], table[1], gots


def reduce_second(state, bits):
    own, last, gots = state
    return call(
        sum_kernel,
        [shape(*own.shape)],
        (own, *gots, hop(last, 1, bits)),
        [VM] * (2 + len(gots)),
        own.size,
        "sum_rows",
    )[0]


def body(
    tokens,
    expert_ids,
    gate_weights,
    request_lengths,
    request_adapter,
    expert_weights,
    expert_down,
    low_down,
    low_up,
):
    experts = lax.axis_size("expert")
    n_dp = lax.axis_size("dp")
    local_tokens, width = tokens.shape
    capacity = local_tokens * TOP * 4 // (3 * experts)
    held = low_down.shape[2] // (2 * RANK)
    adapters = low_up.shape[2] // RANK
    units = expert_down.shape[1]
    bits = []
    b = 2
    while b < n_dp:
        bits.append(b)
        b *= 2
    spots = 1 << len(bits)
    z = lax.axis_index("expert").astype(I32).reshape(1)
    me = lax.axis_index("dp").astype(I32).reshape(1)
    ids_t = expert_ids.T

    outgoing = call(
        functools.partial(front_kernel, experts, capacity),
        [pltpu.HBM((capacity, width + LANES), BF)] * experts,
        (z, *pin([request_lengths, request_adapter, ids_t, tokens])),
        [SM, ANY, ANY, ANY, ANY],
        2 * experts * capacity * local_tokens * width,
        "front",
        [
            pltpu.SMEM(request_lengths.shape, I32),
            pltpu.SMEM(request_adapter.shape, I32),
            pltpu.VMEM(ids_t.shape, I32),
            pltpu.VMEM(tokens.shape, BF),
            pltpu.VMEM((experts, capacity, width + LANES), BF),
            pltpu.SemaphoreType.DMA((4,)),
            pltpu.SemaphoreType.DMA((experts,)),
        ],
        ANY,
    )
    wt_t = jnp.swapaxes(expert_weights[0], 1, 2)
    lu_t = jnp.swapaxes(low_up[0], 1, 2)
    ld_o = swap(low_down[0], "dp", 1)
    wt_o = swap(after(wt_t, outgoing), "dp", 1)
    ld = stage([low_down[0], ld_o], 1, "stage_low_down")
    wt = stage([wt_t, wt_o], 0, "stage_gate_up")
    lanes = 2 * RANK * spots
    fold = (
        jnp.arange(4 * held * RANK)[:, None] % (2 * RANK) == jnp.arange(lanes)[None, :] % (2 * RANK)
    ).astype(BF)
    tile = jnp.stack(
        [
            (
                jnp.arange(lanes)[None, :] % (2 * RANK)
                == jnp.arange(adapters * RANK)[:, None] % RANK + g * RANK
            ).astype(BF)
            for g in range(2)
        ]
    )

    order = list(range(experts))
    first, second = {}, {}
    first[0] = gather_first(outgoing[0], bits)
    arrived = [outgoing[0]] + [swap(outgoing[order[i]], "expert", order[i]) for i in (1, 2)]

    group = capacity
    count = group * spots
    parts, done, adds = {}, {}, {}
    first[0] = after(first[0], (arrived[1], ld_o))
    second[0] = gather_second(first[0], bits)
    lu_o = swap(after(lu_t, (wt_o, first[0])), "dp", 1)
    dn_o = swap(after(expert_down[0], (lu_o, second[0])), "dp", 1)
    lu = stage([lu_t, lu_o], 0, "stage_low_up")
    dn = stage([expert_down[0], dn_o], 0, "stage_down")
    first[1] = gather_first(after(arrived[1], (second[0], wt, ld)), bits)
    last = experts - 1
    backs = [None] * experts

    def give(j):
        backs[order[j]] = done[j] if order[j] == 0 else swap(done[j], "expert", order[j])

    for i, d in enumerate(order):
        deps = [first[2]] if i == 1 else [wt] if i == 0 else []
        if i >= 1:
            deps.append(parts[i - 1][0])
        if i >= 2:
            done[i - 2] = reduce_second(adds[i - 2], bits)
            deps.append(done[i - 2])
            give(i - 2)
        pieces = after(second[i], deps)
        got = call(
            functools.partial(proj_kernel, spots, held),
            [shape(width, count), shape(8, count, F32)] + [shape(group, lanes)] * 2,
            (me, fold, *pin(pieces), ld),
            [SM, VM] + [ANY] * spots + [VM],
            4 * count * width * held * 2 * RANK,
            "project",
            [pltpu.VMEM((count, width + LANES), BF), pltpu.SemaphoreType.DMA((spots,))],
        )
        rows, tags, low, send = got
        deps = [first[1], dn_o] if i == 0 else [second[3]] if i == 2 else []
        if i == 0:
            second[1] = gather_second(after(first[1], low), bits)
            first[2] = gather_first(after(arrived[2], low), bits)
            second[2] = gather_second(first[2], bits)
        rows = after(rows, deps)
        raw = []
        for side in range(2):
            raw.append(
                call(
                    functools.partial(main_kernel, side),
                    [jax.ShapeDtypeStruct((2, units, count), F32)],
                    (rows, wt),
                    [VM] * 2,
                    4 * count * width * units,
                    "gate_up",
                )[0]
            )
            if side == 0:
                recv = hop(send, 1, bits)
                early = raw[0]
                low = after(low, early)
                if i >= 1:
                    adds[i - 1] = reduce_first(parts[i - 1], bits, raw)
                    low = after(low, adds[i - 1][1])
                for j in range(1, len(bits)):
                    low, send = call(
                        functools.partial(mix_kernel, 1 << j),
                        [shape(group, lanes)] * 2,
                        (low, recv),
                        [VM] * 2,
                        group * lanes,
                        "mix",
                    )
                    recv = hop(send, 1 << j, bits)
                rows = after(rows, low)
        if i == 0:
            for j in range(3, experts):
                piece = after(outgoing[order[j]], (arrived[j - 1], early))
                arrived.append(swap(piece, "expert", order[j]))
                first[j] = gather_first(after(arrived[j], raw), bits)
                second[j] = gather_second(first[j], bits)
        deps = [second[1]] if i == 0 else [second[2], first[3]] if i == 1 else []
        raw = after(raw, deps)
        parts[i] = call(
            functools.partial(down_kernel, spots),
            [shape(group, width)] * spots,
            (tile, low, recv, tags, *raw, lu, dn),
            [VM] * 8,
            8 * count * adapters * RANK * units + 4 * count * units * width,
            "down",
        )
    done[last - 1] = reduce_second(adds[last - 1], bits)
    give(last - 1)
    own, left, gots = reduce_first(parts[last], bits)
    own = after(own, [backs[order[i]] for i in range(last)])
    done[last] = reduce_second((own, left, gots), bits)
    give(last)

    return call(
        functools.partial(back_kernel, experts, capacity),
        [shape(local_tokens, width)],
        (z, ids_t, expert_ids, gate_weights, tokens, *backs),
        [SM] + [VM] * (4 + experts),
        2 * experts * capacity * local_tokens * width,
        "combine",
    )[0]


def solution(mesh):
    return jax.shard_map(
        body,
        mesh=mesh,
        in_specs=(
            P(("expert", "dp"), None),
            P(("expert", "dp"), None),
            P(("expert", "dp"), None),
            P(("expert", "dp"), None),
            P(("expert", "dp"), None),
            P("expert", None, None, "dp"),
            P("expert", "dp", None),
            P("expert", None, "dp"),
            P("expert", None, None, "dp"),
        ),
        out_specs=P(("expert", "dp"), None),
        check_vma=False,
    )
```
